256 devices in a mesh: group: 8 (over x, y_lo), dev: 32 (over y_hi, z, core).
Axes of the slice: x: 4, y: 4 (y_hi: 2, y_lo: 2; y = y_hi * 2 + y_lo), z: 8, core: 2. Of those that a mesh axis runs over, the one named last changes fastest.
Arguments:
- particles: float32 [512, 16, 8, 128], P(('group', 'dev')), as said below
- counts: int32 [512, 16], P(('group', 'dev')), may hold values from 0 to 128, as said below
Outputs:
- density: float32 [512, 16, 128], P(('group', 'dev'))
- density_rate: float32 [512, 16, 128], P(('group', 'dev'))
- acceleration: float32 [512, 16, 2, 128], P(('group', 'dev'))
The draws below stay inside these ranges and needn't reach their ends.
Inputs may be any that keep to these rules, and one draw needn't show every extreme that they name: The first counts slots of a cell hold its live particles. `particles`: every slot's mass (component 4) is positive and every smoothing length (component 5) lies within 0.3 to 0.5.
All inputs are finite; a program needn't handle non-finite values.
Results may differ from the reference program's by a relative error of at most 0.0001.
Values sent between devices are 32-bit elements; how exact they have to be, the bound alone decides.
A program may use at most 64 MiB of HBM per device.

```python
import math
import jax
import jax.numpy as jnp
from jax import lax

CY = 16
COMP = 8
SLOTS = 128
GX = 512


def draw_counts(key, part):
    key_height = jax.random.fold_in(key, 11)
    key_fill = jax.random.fold_in(key, 12)
    key_top = jax.random.fold_in(key, 13)
    column_ids = jnp.arange(GX, dtype=jnp.int32)[:, None]
    row_ids = jnp.arange(CY, dtype=jnp.int32)[None, :]
    side_height = jax.random.randint(key_height, (GX, 1), 1, CY // 3 + 2)
    height = jnp.where(column_ids < GX // 4, CY, side_height)
    interior = jax.random.randint(key_fill, (GX, CY), 3 * SLOTS // 4, SLOTS + 1)
    surface = jax.random.randint(key_top, (GX, CY), SLOTS // 8, SLOTS + 1)
    filled = jnp.where(row_ids == 0, SLOTS, jnp.where(row_ids == height - 1, surface, interior))
    return jnp.where(row_ids < height, filled, 0).astype(jnp.int32)


def draw_particles(key, part):
    shape_all = (GX, CY, COMP, SLOTS)
    uniform_draw = jax.random.uniform(jax.random.fold_in(key, 21), shape_all, jnp.float32)
    normal_draw = jax.random.normal(jax.random.fold_in(key, 22), shape_all, jnp.float32)
    position = jnp.arange(GX, dtype=jnp.float32)[:, None, None, None] / GX
    comp_ids = jnp.arange(COMP, dtype=jnp.int32)[None, None, :, None]
    ramp = jnp.exp(math.log(3.0) * position)
    velocity = 0.05 * ramp * normal_draw
    mass = jnp.exp(math.log(0.5) + math.log(4.0) * uniform_draw) / SLOTS
    smoothing = 0.3 + 0.2 * uniform_draw
    rest = 0.3 + 0.9 * uniform_draw
    viscosity = jnp.exp(math.log(0.5) + math.log(5.0) * uniform_draw)
    result = jnp.where(comp_ids < 2, uniform_draw, velocity)
    result = jnp.where(comp_ids == 4, mass, result)
    result = jnp.where(comp_ids == 5, smoothing, result)
    result = jnp.where(comp_ids == 6, rest, result)
    result = jnp.where(comp_ids == 7, viscosity, result)
    return result.astype(jnp.float32)


def setup_inputs(seed: int = 0) -> dict:
    streams_of = jax.random.split(jax.random.key(seed), 3)
    return {
        "particles": draw_particles(jax.random.fold_in(streams_of[2], 71), 0),
        "counts": draw_counts(jax.random.fold_in(streams_of[2], 71), 0),
    }


wendland_norm = 7.0 / (4.0 * math.pi)
gradient_norm = 35.0 / (4.0 * math.pi)
sound_factor = 10.0
visc_softening = 0.01
neighbour_steps = ((-1, -1), (-1, 0), (-1, 1), (0, -1), (0, 0), (0, 1), (1, -1), (1, 0), (1, 1))

def pair_geometry(centre, neighbour, step_x, step_y):
    sep_x = centre[:, 0, :, None] - neighbour[:, 0, None, :] - step_x
    sep_y = centre[:, 1, :, None] - neighbour[:, 1, None, :] - step_y
    pair_h = 0.5 * (centre[:, 5, :, None] + neighbour[:, 5, None, :])
    dist_sq = sep_x * sep_x + sep_y * sep_y
    radius_ratio = jnp.sqrt(dist_sq) / pair_h
    falloff = jnp.maximum(1.0 - 0.5 * radius_ratio, 0.0)
    falloff_cube = falloff * falloff * falloff
    h_square = pair_h * pair_h
    kernel = wendland_norm / h_square * falloff_cube * falloff * (2.0 * radius_ratio + 1.0)
    gradient = -gradient_norm / (h_square * h_square) * falloff_cube
    return (sep_x, sep_y, pair_h, dist_sq, kernel, gradient)

def density_terms(centre, neighbour, step_x, step_y):
    sep_x, sep_y, pair_h, dist_sq, kernel, gradient = pair_geometry(centre, neighbour, step_x, step_y)
    mass_j = neighbour[:, 4, None, :]
    closing = (centre[:, 2, :, None] - neighbour[:, 2, None, :]) * sep_x + (centre[:, 3, :, None] - neighbour[:, 3, None, :]) * sep_y
    return (lax.optimization_barrier(jnp.sum(mass_j * kernel, axis=-1)), lax.optimization_barrier(jnp.sum(mass_j * closing * gradient, axis=-1)))

def force_terms(centre, centre_aux, neighbour, neighbour_aux, step_x, step_y, sound):
    sep_x, sep_y, pair_h, dist_sq, kernel, gradient = pair_geometry(centre, neighbour, step_x, step_y)
    mass_j = neighbour[:, 4, None, :]
    closing = (centre[:, 2, :, None] - neighbour[:, 2, None, :]) * sep_x + (centre[:, 3, :, None] - neighbour[:, 3, None, :]) * sep_y
    approach = jnp.minimum(closing, 0.0) / (dist_sq + visc_softening * pair_h * pair_h)
    alpha_pair = 0.5 * (centre[:, 7, :, None] + neighbour[:, 7, None, :])
    rho_pair = 0.5 * (centre_aux[:, 0, :, None] + neighbour_aux[:, 0, None, :])
    viscous = -alpha_pair * sound * pair_h * approach / rho_pair
    coeff = centre_aux[:, 1, :, None] + neighbour_aux[:, 1, None, :] + viscous
    weight = mass_j * coeff * gradient
    accel_x = -lax.optimization_barrier(jnp.sum(weight * sep_x, axis=-1))
    accel_y = -lax.optimization_barrier(jnp.sum(weight * sep_y, axis=-1))
    return jnp.stack([accel_x, accel_y], axis=1)

def pressure_fields(density_raw, cells, live_slots, sound):
    rho_safe = jnp.where(live_slots, density_raw, 1.0)
    pressure_term = jnp.where(live_slots, sound * sound * (density_raw - cells[:, :, 6, :]) / (rho_safe * rho_safe), 0.0)
    return (rho_safe, pressure_term)

def reference(particles, counts):
    column_total = particles.shape[0]
    row_total = particles.shape[1]
    slot_total = particles.shape[3]
    slot_ids = jnp.arange(slot_total, dtype=jnp.int32)
    live_slots = slot_ids[None, None, :] < counts[:, :, None]
    comp_ids = jnp.arange(particles.shape[2], dtype=jnp.int32)[None, None, :, None]
    masked = jnp.where((comp_ids == 4) & jnp.logical_not(live_slots[:, :, None, :]), 0.0, particles)
    extended = jnp.pad(masked, ((1, 1), (1, 1), (0, 0), (0, 0)))

    def density_column(column_at):
        centre = lax.dynamic_index_in_dim(extended, column_at + 1, 0, keepdims=False)[1:row_total + 1]
        density_sum = jnp.zeros((row_total, slot_total), jnp.float32)
        rate_sum = jnp.zeros((row_total, slot_total), jnp.float32)
        for step_x, step_y in neighbour_steps:
            plane = lax.dynamic_index_in_dim(extended, column_at + 1 + step_x, 0, keepdims=False)
            neighbour = plane[1 + step_y:1 + step_y + row_total]
            density_part, rate_part = density_terms(centre, neighbour, step_x, step_y)
            density_sum = density_sum + density_part
            rate_sum = rate_sum + rate_part
        return (density_sum, rate_sum)
    column_ids = jnp.arange(column_total, dtype=jnp.int32)
    density_raw, rate_raw = lax.map(density_column, column_ids)
    particle_speed = jnp.sqrt(particles[:, :, 2, :] * particles[:, :, 2, :] + particles[:, :, 3, :] * particles[:, :, 3, :])
    sound = sound_factor * jnp.max(jnp.where(live_slots, particle_speed, 0.0))
    rho_safe, pressure_term = pressure_fields(density_raw, masked, live_slots, sound)
    auxiliary = jnp.stack([rho_safe, pressure_term], axis=2)
    aux_extended = jnp.pad(auxiliary, ((1, 1), (1, 1), (0, 0), (0, 0)))

    def force_column(column_at):
        centre = lax.dynamic_index_in_dim(extended, column_at + 1, 0, keepdims=False)[1:row_total + 1]
        centre_aux = lax.dynamic_index_in_dim(aux_extended, column_at + 1, 0, keepdims=False)[1:row_total + 1]
        accel_sum = jnp.zeros((row_total, 2, slot_total), jnp.float32)
        for step_x, step_y in neighbour_steps:
            plane = lax.dynamic_index_in_dim(extended, column_at + 1 + step_x, 0, keepdims=False)
            aux_plane = lax.dynamic_index_in_dim(aux_extended, column_at + 1 + step_x, 0, keepdims=False)
            neighbour = plane[1 + step_y:1 + step_y + row_total]
            neighbour_aux = aux_plane[1 + step_y:1 + step_y + row_total]
            accel_sum = accel_sum + force_terms(centre, centre_aux, neighbour, neighbour_aux, step_x, step_y, sound)
        return accel_sum
    accel_raw = lax.map(force_column, column_ids)
    density = jnp.where(live_slots, density_raw, 0.0)
    density_rate = jnp.where(live_slots, rate_raw, 0.0)
    acceleration = jnp.where(live_slots[:, :, None, :], accel_raw, 0.0)
    return (density, density_rate, acceleration)
```

```python
import functools
import math

import jax
import jax.numpy as jnp
from jax import lax
from jax.experimental import pallas as pl
from jax.experimental.pallas import tpu as pltpu
from jax.sharding import PartitionSpec as P

MESH = pl.DeviceIdType.MESH

kernel_scale = 28.0 / math.pi
gradient_scale = 140.0 / math.pi
sound_factor = 10.0
softening = 0.01 / 4.0
tiny = 1e-30

own_pairs = ((0, 0, 0), (1, 0, 1))
side_pairs = ((2, 1, -1), (3, 1, 0), (4, 1, 1))


def spread_row(row):
    return jnp.broadcast_to(row, (8, row.shape[1]))


def spread_col(col, lanes):
    return jnp.broadcast_to(col, (col.shape[0], lanes))


def column_of(row):
    n = row.shape[1]
    eye = lax.broadcasted_iota(jnp.int32, (n, n), 0) == lax.broadcasted_iota(jnp.int32, (n, n), 1)
    return jnp.sum(jnp.where(eye, jnp.broadcast_to(row, (n, n)), 0.0), axis=1, keepdims=True)


def body(
    sizes,
    p_ref,
    n_ref,
    den_ref,
    rate_ref,
    acc_ref,
    rows_t,
    cols_t,
    aux_rows,
    aux_cols,
    live_t,
    grad_t,
    visc_t,
    acc_i1,
    acc_j1,
    acc_i2,
    acc_j2,
    total_t,
    ghost,
    ghost_n,
    part1_out,
    part1_in,
    rho_out,
    rho_in,
    part2_out,
    part2_in,
    top1,
    top2,
    top_out,
    top2_out,
    send_sem,
    recv_sem,
    top1_send,
    top1_recv,
    top2_send,
    top2_recv,
):
    n_group, n_dev, block, unroll = sizes
    total = n_group * n_dev
    blocks = total // block
    n_cols, n_rows, _, slots = p_ref.shape
    me = lax.axis_index("group") * n_dev + lax.axis_index("dev")

    def coords(flat):
        return (flat // n_dev, flat % n_dev)

    right = coords((me + 1) % total)
    left = coords((me + total - 1) % total)
    offset = me % block
    which = me // block
    near = [coords(which * block + (offset + k) % block) for k in range(1, block)]
    far = [coords(((which + k) % blocks) * block + offset) for k in range(1, blocks)]

    barrier = pltpu.get_barrier_semaphore()
    for other in [left, right] + near + far:
        pl.semaphore_signal(barrier, inc=1, device_id=other, device_id_type=MESH)

    def copy_to(src, dst, send, recv, device):
        return pltpu.make_async_remote_copy(
            src_ref=src,
            dst_ref=dst,
            send_sem=send,
            recv_sem=recv,
            device_id=device,
            device_id_type=MESH,
        )

    ghost_copy = copy_to(p_ref.at[0], ghost, send_sem.at[0], recv_sem.at[0], left)
    count_copy = copy_to(n_ref, ghost_n, send_sem.at[1], recv_sem.at[1], left)
    part1_copy = copy_to(part1_out, part1_in, send_sem.at[2], recv_sem.at[2], right)
    rho_copy = copy_to(rho_out, rho_in, send_sem.at[3], recv_sem.at[3], left)
    part2_copy = copy_to(part2_out, part2_in, send_sem.at[4], recv_sem.at[4], right)

    lane_ids = lax.broadcasted_iota(jnp.int32, (n_rows, slots), 1).astype(jnp.float32)
    mass_row = lax.broadcasted_iota(jnp.int32, (8, slots), 0) == 4

    def live_of(counts_row):
        fill = column_of(counts_row.astype(jnp.float32))
        return jnp.where(lane_ids < fill, 1.0, 0.0)

    def load_cell(c, r, tile):
        live = spread_row(live_t[c, pl.ds(r, 1), :])
        return jnp.where(mass_row & (live < 0.5), 0.0, tile)

    for c in range(n_cols):
        live_t[c] = live_of(n_ref[c : c + 1, :])
    pad = jnp.where(mass_row, 0.0, 0.5)
    for c in range(n_cols + 1):
        rows_t[c, 0] = pad
        rows_t[c, n_rows + 1] = pad
        aux_rows[c, 0] = jnp.ones((8, slots), jnp.float32)
        aux_rows[c, n_rows + 1] = jnp.ones((8, slots), jnp.float32)
    acc_i1[...] = jnp.zeros_like(acc_i1)
    acc_i2[...] = jnp.zeros_like(acc_i2)

    for c in range(n_cols):

        def own_cell(r, carry, c=c):
            tile = load_cell(c, r, p_ref[c, r])
            rows_t[c, r + 1] = tile
            cols_t[c, r] = tile.T
            return carry

        lax.fori_loop(0, n_rows, own_cell, 0)

    top = jnp.zeros((n_rows, slots), jnp.float32)
    for c in range(n_cols):
        vx, vy = (p_ref[c, :, 2, :], p_ref[c, :, 3, :])
        top = jnp.maximum(top, jnp.where(live_t[c] > 0.5, vx * vx + vy * vy, 0.0))
    top_row = spread_row(jnp.max(top, axis=0, keepdims=True))
    top_out[...] = top_row
    top1[offset] = top_row

    def first_pass(c, pairs, first):
        def one_row(r, carry):
            def one_group(step, sums):
                sums = list(sums)
                for u in range(unroll):
                    at = pl.multiple_of((step * unroll + u) * 8, 8)
                    t = cols_t[c, r, pl.ds(at, 8), :]
                    xj, yj, vxj, vyj, mj, hj, cj = [
                        spread_col(t[:, k : k + 1], slots) for k in (0, 1, 2, 3, 4, 5, 7)
                    ]
                    sum_w = sum_r = None
                    for n, (slot, dc, dr) in enumerate(pairs):
                        cell = rows_t.at[c + dc, r + 1 + dr]
                        xi, yi, vxi, vyi, mi, hi, ci = [
                            spread_row(cell[k : k + 1, :]) for k in (0, 1, 2, 3, 4, 5, 7)
                        ]
                        dx = xi - (xj - dc) if dc else xi - xj
                        dy = yi - (yj - dr) if dr else yi - yj
                        inv = 1.0 / (hi + hj)
                        inv_sq = inv * inv
                        ratio_sq = (dx * dx + dy * dy) * inv_sq
                        ratio = ratio_sq * lax.rsqrt(jnp.maximum(ratio_sq, tiny))
                        fall = jnp.maximum(1.0 - ratio, 0.0)
                        base = fall * fall * fall * inv_sq * (mi * mj)
                        grad = base * inv_sq
                        kern = base * (fall * (1.25 - fall))
                        closing = (vxi - vxj) * dx + (vyi - vyj) * dy
                        rate = closing * grad
                        visc = jnp.minimum(rate, 0.0) * ((ci + cj) * inv)
                        visc = visc * (1.0 / (ratio_sq + softening))
                        grad_t[c, r, slot, pl.ds(at, 8), :] = grad
                        visc_t[c, r, slot, pl.ds(at, 8), :] = visc
                        sums[2 * n] = sums[2 * n] + kern
                        sums[2 * n + 1] = sums[2 * n + 1] + rate
                        if slot:
                            sum_w = kern if sum_w is None else sum_w + kern
                            sum_r = rate if sum_r is None else sum_r + rate
                    if first:
                        acc_j1[c, r, 0, pl.ds(at, 8), :] = sum_w
                        acc_j1[c, r, 1, pl.ds(at, 8), :] = sum_r
                    else:
                        acc_j1[c, r, 0, pl.ds(at, 8), :] += sum_w
                        acc_j1[c, r, 1, pl.ds(at, 8), :] += sum_r
                return tuple(sums)

            zero = jnp.zeros((8, slots), jnp.float32)
            sums = lax.fori_loop(0, slots // 8 // unroll, one_group, (zero,) * (2 * len(pairs)))
            for n, (slot, dc, dr) in enumerate(pairs):
                acc_i1[c + dc, r + 1 + dr, 0] += sums[2 * n]
                acc_i1[c + dc, r + 1 + dr, 1] += sums[2 * n + 1]
            return carry

        lax.fori_loop(0, n_rows, one_row, 0)

    def second_pass(c, pairs, first):
        def one_row(r, carry):
            def one_group(step, sums):
                sums = list(sums)
                for u in range(unroll):
                    at = pl.multiple_of((step * unroll + u) * 8, 8)
                    t = cols_t[c, r, pl.ds(at, 8), :]
                    a = aux_cols[c, r, pl.ds(at, 8), :]
                    xj, yj = [spread_col(t[:, k : k + 1], slots) for k in (0, 1)]
                    rho_j, press_j = [spread_col(a[:, k : k + 1], slots) for k in (0, 1)]
                    sum_x = sum_y = None
                    for n, (slot, dc, dr) in enumerate(pairs):
                        cell = rows_t.at[c + dc, r + 1 + dr]
                        aux = aux_rows.at[c + dc, r + 1 + dr]
                        xi, yi = [spread_row(cell[k : k + 1, :]) for k in (0, 1)]
                        rho_i, press_i = [spread_row(aux[k : k + 1, :]) for k in (0, 1)]
                        dx = xi - (xj - dc) if dc else xi - xj
                        dy = yi - (yj - dr) if dr else yi - yj
                        grad = grad_t[c, r, slot, pl.ds(at, 8), :]
                        visc = visc_t[c, r, slot, pl.ds(at, 8), :]
                        force = (press_i + press_j) * grad + visc * (1.0 / (rho_i + rho_j))
                        fx, fy = (force * dx, force * dy)
                        sums[2 * n] = sums[2 * n] + fx
                        sums[2 * n + 1] = sums[2 * n + 1] + fy
                        if slot:
                            sum_x = fx if sum_x is None else sum_x + fx
                            sum_y = fy if sum_y is None else sum_y + fy
                    if first:
                        acc_j2[c, r, 0, pl.ds(at, 8), :] = sum_x
                        acc_j2[c, r, 1, pl.ds(at, 8), :] = sum_y
                    else:
                        acc_j2[c, r, 0, pl.ds(at, 8), :] += sum_x
                        acc_j2[c, r, 1, pl.ds(at, 8), :] += sum_y
                return tuple(sums)

            zero = jnp.zeros((8, slots), jnp.float32)
            sums = lax.fori_loop(0, slots // 8 // unroll, one_group, (zero,) * (2 * len(pairs)))
            for n, (slot, dc, dr) in enumerate(pairs):
                acc_i2[c + dc, r + 1 + dr, 0] += sums[2 * n]
                acc_i2[c + dc, r + 1 + dr, 1] += sums[2 * n + 1]
            return carry

        lax.fori_loop(0, n_rows, one_row, 0)

    def cell_totals(c, acc_i, acc_j, sign):
        def one_row(r, carry):
            for k in range(2):
                other = acc_j[c, r, k].T.reshape(slots // 8, 8, slots).sum(axis=0)
                both = acc_i[c, r + 1, k] + sign * other
                total_t[k, pl.ds(r, 1), :] = jnp.sum(both, axis=0, keepdims=True)
            return carry

        lax.fori_loop(0, n_rows, one_row, 0)

    def ghost_totals(acc_i, out):
        def one_row(r, carry):
            for k in range(2):
                out[k, pl.ds(r, 1), :] = jnp.sum(acc_i[n_cols, r + 1, k], axis=0, keepdims=True)
            return carry

        lax.fori_loop(0, n_rows, one_row, 0)

    def store_aux(c, rho, press, own):
        total_t[0] = rho
        total_t[1] = press

        def one_row(r, carry):
            aux_rows[c, r + 1, 0:1, :] = total_t[0, pl.ds(r, 1), :]
            aux_rows[c, r + 1, 1:2, :] = total_t[1, pl.ds(r, 1), :]
            if own:
                aux_cols[c, r] = aux_rows[c, r + 1].T
            return carry

        lax.fori_loop(0, n_rows, one_row, 0)

    def finish_density(c, extra):
        cell_totals(c, acc_i1, acc_j1, 1.0)
        live = live_t[c] > 0.5
        over_mass = 1.0 / p_ref[c, :, 4, :]
        w, rate = (total_t[0], total_t[1])
        if extra is not None:
            w, rate = (w + extra[0], rate + extra[1])
        rho = w * over_mass * kernel_scale
        den_ref[c] = jnp.where(live, rho, 0.0)
        rate_ref[c] = jnp.where(live, rate * over_mass * (-gradient_scale), 0.0)
        return jnp.where(live, rho, 1.0)

    def pressure(rho, rest, live, sound):
        return jnp.where(live > 0.5, (-2.0 * sound) * (rho - rest) / (rho * rho), 0.0)

    def finish_force(c, extra, sound):
        cell_totals(c, acc_i2, acc_j2, -1.0)
        live = live_t[c] > 0.5
        scale = (-0.5 * gradient_scale * sound) / p_ref[c, :, 4, :]
        for k in range(2):
            value = total_t[k]
            if extra is not None:
                value = value + extra[k]
            acc_ref[c, :, k, :] = jnp.where(live, value * scale, 0.0)

    last = n_cols - 1

    pl.semaphore_wait(barrier, 2 + len(near) + len(far))
    ghost_copy.start()
    count_copy.start()
    near_copies = [
        copy_to(top_out, top1.at[offset], top1_send.at[k], top1_recv.at[offset], other)
        for k, other in enumerate(near)
    ]
    for copy in near_copies:
        copy.start()

    for c in range(n_cols):
        if c < last:
            first_pass(c, own_pairs, True)

    for k in range(1, block):
        sender = (offset + k) % block
        copy_to(top_out, top1.at[sender], top1_send.at[k - 1], top1_recv.at[sender], left).wait_recv()
    block_top = top1[0]
    for k in range(1, block):
        block_top = jnp.maximum(block_top, top1[k])
    top2_out[...] = block_top
    top2[which] = block_top
    far_copies = [
        copy_to(top2_out, top2.at[which], top2_send.at[k], top2_recv.at[which], other)
        for k, other in enumerate(far)
    ]
    for copy in far_copies:
        copy.start()

    ghost_copy.wait_recv()
    count_copy.wait_recv()
    inside = jnp.where(me < total - 1, 1.0, 0.0)
    live_t[n_cols] = live_of(ghost_n[0:1, :]) * inside

    def ghost_cell(r, carry):
        rows_t[n_cols, r + 1] = load_cell(n_cols, r, ghost[r])
        return carry

    lax.fori_loop(0, n_rows, ghost_cell, 0)

    first_pass(last, side_pairs, True)
    ghost_totals(acc_i1, part1_out)
    part1_copy.start()
    for c in range(last):
        first_pass(c, side_pairs, False)

    for k in range(1, blocks):
        sender = (which + k) % blocks
        copy_to(top2_out, top2.at[sender], top2_send.at[k - 1], top2_recv.at[sender], left).wait_recv()
    all_top = top2[0]
    for k in range(1, blocks):
        all_top = jnp.maximum(all_top, top2[k])
    all_top = jnp.max(all_top, axis=1, keepdims=True)
    sound_col = sound_factor * jnp.sqrt(all_top)
    sound = jnp.broadcast_to(sound_col[0:1, :], (n_rows, slots))

    part1_copy.wait_recv()
    for c in range(last):
        rho = finish_density(c, part1_in if c == 0 else None)
        if c == 0:
            rho_out[...] = rho
            rho_copy.start()
        store_aux(c, rho, pressure(rho, p_ref[c, :, 6, :], live_t[c], sound), True)
    first_pass(last, own_pairs, False)
    rho = finish_density(last, None)
    store_aux(last, rho, pressure(rho, p_ref[last, :, 6, :], live_t[last], sound), True)

    for c in range(last):
        second_pass(c, own_pairs, True)
    rho_copy.wait_recv()
    rho = rho_in[...]
    store_aux(n_cols, rho, pressure(rho, ghost[:, 6, :], live_t[n_cols], sound), False)
    second_pass(last, side_pairs, True)
    ghost_totals(acc_i2, part2_out)
    part2_copy.start()
    for c in range(last):
        second_pass(c, side_pairs, False)
    second_pass(last, own_pairs, False)
    finish_force(last, None, sound)
    part2_copy.wait_recv()
    for c in range(last):
        finish_force(c, part2_in if c == 0 else None, sound)

    for copy in [ghost_copy, count_copy, part1_copy, rho_copy, part2_copy] + near_copies + far_copies:
        copy.wait_send()


def on_device(sizes, particles, counts):
    n_group, n_dev, block, _ = sizes
    blocks = n_group * n_dev // block
    n_cols, n_rows, comps, slots = particles.shape
    f32 = jnp.float32
    vmem = pl.BlockSpec(memory_space=pltpu.VMEM)
    pair_store = pltpu.VMEM((n_cols, n_rows, 5, slots, slots), f32)
    acc_i = pltpu.VMEM((n_cols + 1, n_rows + 2, 2, 8, slots), f32)
    acc_j = pltpu.VMEM((n_cols, n_rows, 2, slots, slots), f32)
    pair_rows = pltpu.VMEM((2, n_rows, slots), f32)
    return pl.pallas_call(
        functools.partial(body, sizes),
        out_shape=(
            jax.ShapeDtypeStruct((n_cols, n_rows, slots), f32),
            jax.ShapeDtypeStruct((n_cols, n_rows, slots), f32),
            jax.ShapeDtypeStruct((n_cols, n_rows, 2, slots), f32),
        ),
        in_specs=[vmem, vmem],
        out_specs=(vmem, vmem, vmem),
        scratch_shapes=[
            pltpu.VMEM((n_cols + 1, n_rows + 2, 8, slots), f32),
            pltpu.VMEM((n_cols, n_rows, slots, 8), f32),
            pltpu.VMEM((n_cols + 1, n_rows + 2, 8, slots), f32),
            pltpu.VMEM((n_cols, n_rows, slots, 8), f32),
            pltpu.VMEM((n_cols + 1, n_rows, slots), f32),
            pair_store,
            pair_store,
            acc_i,
            acc_j,
            acc_i,
            acc_j,
            pair_rows,
            pltpu.VMEM((n_rows, 8, slots), f32),
            pltpu.VMEM(counts.shape, jnp.int32),
            pair_rows,
            pair_rows,
            pltpu.VMEM((n_rows, slots), f32),
            pltpu.VMEM((n_rows, slots), f32),
            pair_rows,
            pair_rows,
            pltpu.VMEM((block, 8, slots), f32),
            pltpu.VMEM((blocks, 8, slots), f32),
            pltpu.VMEM((8, slots), f32),
            pltpu.VMEM((8, slots), f32),
            pltpu.SemaphoreType.DMA((5,)),
            pltpu.SemaphoreType.DMA((5,)),
            pltpu.SemaphoreType.DMA((block,)),
            pltpu.SemaphoreType.DMA((block,)),
            pltpu.SemaphoreType.DMA((blocks,)),
            pltpu.SemaphoreType.DMA((blocks,)),
        ],
        compiler_params=pltpu.CompilerParams(
            collective_id=0, has_side_effects=True, vmem_limit_bytes=60 * 1024 * 1024
        ),
        name="sph",
    )(particles, counts)


def solution(mesh):
    n_group, n_dev = (mesh.shape["group"], mesh.shape["dev"])
    block = 1
    while block * block * 4 <= n_group * n_dev:
        block *= 2
    return jax.shard_map(
        functools.partial(on_device, (n_group, n_dev, block, 4)),
        mesh=mesh,
        in_specs=(P(("group", "dev"), None, None, None), P(("group", "dev"), None)),
        out_specs=(
            P(("group", "dev"), None, None),
            P(("group", "dev"), None, None),
            P(("group", "dev"), None, None, None),
        ),
        check_vma=False,
    )
```

```python
import functools
import math

import jax
import jax.numpy as jnp
from jax import lax
from jax.experimental import pallas as pl
from jax.experimental.pallas import tpu as pltpu
from jax.sharding import PartitionSpec as P

MESH = pl.DeviceIdType.MESH

kernel_scale = 28.0 / math.pi
gradient_scale = 140.0 / math.pi
sound_factor = 10.0
softening = 0.01 / 4.0
tiny = 1e-30

own_pairs = ((0, 0, 0), (1, 0, 1))
side_pairs = ((2, 1, -1), (3, 1, 0), (4, 1, 1))


def spread_row(row):
    return jnp.broadcast_to(row, (8, row.shape[1]))


def column_of(row):
    n = row.shape[1]
    eye = lax.broadcasted_iota(jnp.int32, (n, n), 0) == lax.broadcasted_iota(jnp.int32, (n, n), 1)
    return jnp.sum(jnp.where(eye, jnp.broadcast_to(row, (n, n)), 0.0), axis=1, keepdims=True)


def split(value):
    high = value.astype(jnp.bfloat16).astype(jnp.float32)
    rest = value - high
    middle = rest.astype(jnp.bfloat16).astype(jnp.float32)
    return (high, middle, rest - middle)


def body(
    sizes,
    p_ref,
    n_ref,
    den_ref,
    rate_ref,
    acc_ref,
    mean_t,
    lhs1,
    lhs2,
    moved,
    fixed,
    steps,
    sums_t,
    geo1,
    geo2,
    live_t,
    grad_t,
    visc_t,
    acc_i1,
    acc_j1,
    acc_i2,
    acc_j2,
    total_t,
    ghost,
    ghost_n,
    part1_out,
    part1_in,
    rho_out,
    rho_in,
    part2_out,
    part2_in,
    top1,
    top2,
    top_out,
    top2_out,
    send_sem,
    recv_sem,
    top1_send,
    top1_recv,
    top2_send,
    top2_recv,
):
    n_group, n_dev, block = sizes
    total = n_group * n_dev
    blocks = total // block
    n_cols, n_rows, _, slots = p_ref.shape
    me = lax.axis_index("group") * n_dev + lax.axis_index("dev")

    def coords(flat):
        return (flat // n_dev, flat % n_dev)

    right = coords((me + 1) % total)
    left = coords((me + total - 1) % total)
    offset = me % block
    which = me // block
    near = [coords(which * block + (offset + k) % block) for k in range(1, block)]
    far = [coords(((which + k) % blocks) * block + offset) for k in range(1, blocks)]

    barrier = pltpu.get_barrier_semaphore()
    for other in [left, right] + near + far:
        pl.semaphore_signal(barrier, inc=1, device_id=other, device_id_type=MESH)

    def copy_to(src, dst, send, recv, device):
        return pltpu.make_async_remote_copy(
            src_ref=src,
            dst_ref=dst,
            send_sem=send,
            recv_sem=recv,
            device_id=device,
            device_id_type=MESH,
        )

    ghost_copy = copy_to(p_ref.at[0], ghost, send_sem.at[0], recv_sem.at[0], left)
    count_copy = copy_to(n_ref, ghost_n, send_sem.at[1], recv_sem.at[1], left)
    part1_copy = copy_to(part1_out, part1_in, send_sem.at[2], recv_sem.at[2], right)
    rho_copy = copy_to(rho_out, rho_in, send_sem.at[3], recv_sem.at[3], left)
    part2_copy = copy_to(part2_out, part2_in, send_sem.at[4], recv_sem.at[4], right)

    lane_ids = lax.broadcasted_iota(jnp.int32, (n_rows, slots), 1).astype(jnp.float32)
    mass_row = lax.broadcasted_iota(jnp.int32, (8, slots), 0) == 4

    def live_of(counts_row):
        fill = column_of(counts_row.astype(jnp.float32))
        return jnp.where(lane_ids < fill, 1.0, 0.0)

    row_ids = lax.broadcasted_iota(jnp.int32, (8, slots), 0)
    zeros = jnp.zeros((8, slots), jnp.float32)
    zeros16 = jnp.zeros((16, slots), jnp.bfloat16)

    def pick(k, value, other):
        return jnp.where(row_ids == k, value, other)

    def pair_up(a, b):
        return jnp.concatenate([a, b], axis=0).astype(jnp.bfloat16)

    def load_cell(c, r, tile):
        live = spread_row(live_t[c, pl.ds(r, 1), :])
        tile = jnp.where(mass_row & (live < 0.5), 0.0, tile)
        return tile - mean_t[...]

    def square_sums(tile):
        square = tile * tile
        turned = pltpu.roll(tile, 6, axis=0)
        work = tile * turned
        return (
            spread_row(square[0:1, :] + square[1:2, :]),
            spread_row(work[0:1, :] + work[1:2, :]),
            turned,
        )

    def lane_side(c, row, tile, kinds):
        at_six = [spread_row(tile[k : k + 1, :]) for k in (5, 7)]
        plain = (
            pick(5, 1.0, pick(6, at_six[0], 0.0)),
            pick(7, 1.0, pick(6, at_six[1], 0.0)),
            pick(4, tile, 0.0),
        )
        for q, value in enumerate(plain):
            for level, part in enumerate(split(value)):
                fixed[c, row, q, level] = pair_up(part, zeros)
        for slot, dc, dr in kinds:
            here = tile + pick(0, float(dc), pick(1, float(dr), 0.0))
            size, work, turned = square_sums(here)
            back = pltpu.roll(here, 2, axis=0)
            for_size = jnp.where(row_ids < 2, -2.0 * here, pick(6, size, 0.0))
            for_work = jnp.where(
                row_ids < 2, -turned, jnp.where(row_ids < 4, -back, pick(6, work, 0.0))
            )
            for q, value in enumerate((for_size, for_work)):
                for level, part in enumerate(split(value)):
                    extra = pick(q, 1.0, 0.0) if level == 0 else zeros
                    moved[c, row, slot, q, level] = pair_up(part, extra)
            for q in range(2):
                parts = split(spread_row(here[q : q + 1, :]))
                parts = [pick(q, -1.0, pick(4, part, 0.0)) for part in parts]
                steps[c, row, slot, q, 0:16] = pair_up(parts[0], parts[1])
                steps[c, row, slot, q, 16:32] = pair_up(parts[2], zeros)

    def sublane_side(c, r, tile):
        size, work, _ = square_sums(tile)
        first = split(pick(6, 1.0, tile))
        second = split(pick(0, size, pick(1, work, 0.0)))
        levels = [jnp.concatenate([a, b], axis=0) for a, b in zip(first, second)]
        stack = [levels[k] for k in (0, 0, 0, 1, 1, 2)]
        stack = stack + [jnp.zeros((slots - 96, slots), jnp.float32)]
        lhs1[c, r] = jnp.concatenate(stack, axis=0).T.astype(jnp.bfloat16)

    def first_rhs(c, row, slot):
        parts = []
        for q in range(5):
            if q < 2:
                levels = [moved[c, row, slot, q, k] for k in range(3)]
            else:
                levels = [fixed[c, row, q - 2, k] for k in range(3)]
            stack = [levels[k] for k in (0, 1, 2, 0, 1, 0)] + [zeros16] * ((slots - 96) // 16)
            parts.append(jnp.concatenate(stack, axis=0))
        return jnp.concatenate(parts, axis=1)

    def second_rhs(c, row, slot):
        fill = [zeros16] * ((slots - 32) // 16)
        parts = [jnp.concatenate([steps[c, row, slot, q]] + fill, axis=0) for q in range(2)]
        parts += [jnp.concatenate([sums_t[c, row, q]] + fill, axis=0) for q in range(2)]
        return jnp.concatenate(parts, axis=1)

    for c in range(n_cols):
        live_t[c] = live_of(n_ref[c : c + 1, :])
    top = jnp.zeros((n_rows, slots), jnp.float32)
    count = jnp.zeros((n_rows, slots), jnp.float32)
    mean_x = jnp.zeros((n_rows, slots), jnp.float32)
    mean_y = jnp.zeros((n_rows, slots), jnp.float32)
    for c in range(n_cols):
        vx, vy = (p_ref[c, :, 2, :], p_ref[c, :, 3, :])
        live = live_t[c]
        top = jnp.maximum(top, jnp.where(live > 0.5, vx * vx + vy * vy, 0.0))
        count = count + live
        mean_x = mean_x + live * vx
        mean_y = mean_y + live * vy
    top_row = spread_row(jnp.max(top, axis=0, keepdims=True))

    def whole_sum(value):
        lanes = jnp.sum(value, axis=0, keepdims=True)
        return jnp.broadcast_to(jnp.sum(spread_row(lanes), axis=1, keepdims=True), (8, slots))

    share = 1.0 / jnp.maximum(whole_sum(count), 1.0)
    mean_t[...] = jnp.where(
        row_ids < 2,
        0.5,
        pick(2, whole_sum(mean_x) * share, pick(3, whole_sum(mean_y) * share, 0.0)),
    )
    pad = pick(5, 0.5, 0.0)
    kinds_of = {}
    for c in range(n_cols + 1):
        kinds = own_pairs if c == 0 else side_pairs if c == n_cols else own_pairs + side_pairs
        kinds_of[c] = kinds
        for row in (0, n_rows + 1):
            lane_side(c, row, pad, kinds)
            for q in range(2):
                parts = [pick(2 + q, 1.0, pick(4, 1.0 if k == 0 and q == 0 else 0.0, 0.0)) for k in range(3)]
                sums_t[c, row, q, 0:16] = pair_up(parts[0], parts[1])
                sums_t[c, row, q, 16:32] = pair_up(parts[2], zeros)
    acc_i1[...] = jnp.zeros_like(acc_i1)
    acc_i2[...] = jnp.zeros_like(acc_i2)

    for c in range(n_cols):

        def own_cell(r, carry, c=c):
            tile = load_cell(c, r, p_ref[c, r])
            lane_side(c, r + 1, tile, kinds_of[c])
            sublane_side(c, r, tile)
            return carry

        lax.fori_loop(0, n_rows, own_cell, 0)

    top_out[...] = top_row
    top1[offset] = top_row

    def run_pairs(c, pairs, lhs, rhs, geo, use):
        depth = len(pairs)

        def fill(r, n):
            slot, dc, dr = pairs[n]
            width = geo.shape[1]
            out = jnp.dot(
                lhs[c, r], rhs(c + dc, r + 1 + dr, slot), preferred_element_type=jnp.float32
            )
            for q in range(width):
                geo[n, q] = out[:, q * slots : (q + 1) * slots]

        def one_row(r, carry):
            for n in range(depth):
                if n + 1 < depth:
                    fill(r, n + 1)
                else:
                    fill(jnp.minimum(r + 1, n_rows - 1), 0)
                use(r, n)
            return carry

        fill(0, 0)
        lax.fori_loop(0, n_rows, one_row, 0)

    def first_pass(c, pairs, first):
        def use(r, n):
            slot, dc, dr = pairs[n]
            total_w = total_r = zeros
            for g in range(slots // 8):
                at = slice(g * 8, g * 8 + 8)
                size, closing, reach, coeff, mass = [geo1[n, q, at, :] for q in range(5)]
                inv = 1.0 / reach
                inv_sq = inv * inv
                ratio_sq = jnp.maximum(size * inv_sq, tiny)
                ratio = ratio_sq * lax.rsqrt(ratio_sq)
                fall = jnp.maximum(1.0 - ratio, 0.0)
                base = fall * fall * fall * (inv_sq * mass)
                grad = base * inv_sq
                kern = base * (fall * (1.25 - fall))
                rate = closing * grad
                visc = jnp.minimum(rate, 0.0) * (coeff * inv)
                visc = visc * (1.0 / (ratio_sq + softening))
                grad_t[c, r, slot, at, :] = grad
                visc_t[c, r, slot, at, :] = visc
                total_w = total_w + kern
                total_r = total_r + rate
                if slot:
                    if first and n == (1 if slot == 1 else 0):
                        acc_j1[c, r, 0, at, :] = kern
                        acc_j1[c, r, 1, at, :] = rate
                    else:
                        acc_j1[c, r, 0, at, :] += kern
                        acc_j1[c, r, 1, at, :] += rate
            acc_i1[c + dc, r + 1 + dr, 0] += total_w
            acc_i1[c + dc, r + 1 + dr, 1] += total_r

        run_pairs(c, pairs, lhs1, first_rhs, geo1, use)

    def second_pass(c, pairs, first):
        def use(r, n):
            slot, dc, dr = pairs[n]
            total_x = total_y = zeros
            for g in range(slots // 8):
                at = slice(g * 8, g * 8 + 8)
                dx, dy, rho, press = [geo2[n, q, at, :] for q in range(4)]
                force = press * grad_t[c, r, slot, at, :] + visc_t[c, r, slot, at, :] * (1.0 / rho)
                fx, fy = (force * dx, force * dy)
                total_x = total_x + fx
                total_y = total_y + fy
                if slot:
                    if first and n == (1 if slot == 1 else 0):
                        acc_j2[c, r, 0, at, :] = fx
                        acc_j2[c, r, 1, at, :] = fy
                    else:
                        acc_j2[c, r, 0, at, :] += fx
                        acc_j2[c, r, 1, at, :] += fy
            acc_i2[c + dc, r + 1 + dr, 0] += total_x
            acc_i2[c + dc, r + 1 + dr, 1] += total_y

        run_pairs(c, pairs, lhs2, second_rhs, geo2, use)

    def cell_totals(c, acc_i, acc_j, sign):
        def one_row(r, carry):
            for k in range(2):
                other = acc_j[c, r, k].T.reshape(slots // 8, 8, slots).sum(axis=0)
                both = acc_i[c, r + 1, k] + sign * other
                total_t[k, pl.ds(r, 1), :] = jnp.sum(both, axis=0, keepdims=True)
            return carry

        lax.fori_loop(0, n_rows, one_row, 0)

    def ghost_totals(acc_i, out):
        def one_row(r, carry):
            for k in range(2):
                out[k, pl.ds(r, 1), :] = jnp.sum(acc_i[n_cols, r + 1, k], axis=0, keepdims=True)
            return carry

        lax.fori_loop(0, n_rows, one_row, 0)

    def store_aux(c, rho, press, own):
        total_t[0] = rho
        total_t[1] = press

        def one_row(r, carry):
            both = [total_t[k, pl.ds(r, 1), :] for k in range(2)]
            for q in range(2):
                parts = split(spread_row(both[q]))
                parts = [pick(2 + q, 1.0, pick(4, part, 0.0)) for part in parts]
                sums_t[c, r + 1, q, 0:16] = pair_up(parts[0], parts[1])
                sums_t[c, r + 1, q, 16:32] = pair_up(parts[2], zeros)
            if own:
                tile = p_ref[c, r] - mean_t[...]
                tile = jnp.where(row_ids < 2, tile, 0.0)
                tile = pick(2, spread_row(both[0]), pick(3, spread_row(both[1]), tile))
                parts = [pick(4, 1.0, part) for part in split(tile)]
                stack = parts + [jnp.zeros((slots - 24, slots), jnp.float32)]
                lhs2[c, r] = jnp.concatenate(stack, axis=0).T.astype(jnp.bfloat16)
            return carry

        lax.fori_loop(0, n_rows, one_row, 0)

    def finish_density(c, extra):
        cell_totals(c, acc_i1, acc_j1, 1.0)
        live = live_t[c] > 0.5
        over_mass = 1.0 / p_ref[c, :, 4, :]
        w, rate = (total_t[0], total_t[1])
        if extra is not None:
            w, rate = (w + extra[0], rate + extra[1])
        rho = w * over_mass * kernel_scale
        den_ref[c] = jnp.where(live, rho, 0.0)
        rate_ref[c] = jnp.where(live, rate * over_mass * (-gradient_scale), 0.0)
        return jnp.where(live, rho, 1.0)

    def pressure(rho, rest, live, sound):
        return jnp.where(live > 0.5, (-2.0 * sound) * (rho - rest) / (rho * rho), 0.0)

    def finish_force(c, extra, sound):
        cell_totals(c, acc_i2, acc_j2, -1.0)
        live = live_t[c] > 0.5
        scale = (-0.5 * gradient_scale * sound) / p_ref[c, :, 4, :]
        for k in range(2):
            value = total_t[k]
            if extra is not None:
                value = value + extra[k]
            acc_ref[c, :, k, :] = jnp.where(live, value * scale, 0.0)

    last = n_cols - 1

    pl.semaphore_wait(barrier, 2 + len(near) + len(far))
    ghost_copy.start()
    count_copy.start()
    near_copies = [
        copy_to(top_out, top1.at[offset], top1_send.at[k], top1_recv.at[offset], other)
        for k, other in enumerate(near)
    ]
    for copy in near_copies:
        copy.start()

    for c in range(n_cols):
        if c < last:
            first_pass(c, own_pairs, True)

    for k in range(1, block):
        sender = (offset + k) % block
        copy_to(top_out, top1.at[sender], top1_send.at[k - 1], top1_recv.at[sender], left).wait_recv()
    block_top = top1[0]
    for k in range(1, block):
        block_top = jnp.maximum(block_top, top1[k])
    top2_out[...] = block_top
    top2[which] = block_top
    far_copies = [
        copy_to(top2_out, top2.at[which], top2_send.at[k], top2_recv.at[which], other)
        for k, other in enumerate(far)
    ]
    for copy in far_copies:
        copy.start()

    ghost_copy.wait_recv()
    count_copy.wait_recv()
    inside = jnp.where(me < total - 1, 1.0, 0.0)
    live_t[n_cols] = live_of(ghost_n[0:1, :]) * inside

    def ghost_cell(r, carry):
        lane_side(n_cols, r + 1, load_cell(n_cols, r, ghost[r]), kinds_of[n_cols])
        return carry

    lax.fori_loop(0, n_rows, ghost_cell, 0)

    first_pass(last, side_pairs, True)
    ghost_totals(acc_i1, part1_out)
    part1_copy.start()
    for c in range(last):
        first_pass(c, side_pairs, False)

    for k in range(1, blocks):
        sender = (which + k) % blocks
        copy_to(top2_out, top2.at[sender], top2_send.at[k - 1], top2_recv.at[sender], left).wait_recv()
    all_top = top2[0]
    for k in range(1, blocks):
        all_top = jnp.maximum(all_top, top2[k])
    all_top = jnp.max(all_top, axis=1, keepdims=True)
    sound_col = sound_factor * jnp.sqrt(all_top)
    sound = jnp.broadcast_to(sound_col[0:1, :], (n_rows, slots))

    part1_copy.wait_recv()
    for c in range(last):
        rho = finish_density(c, part1_in if c == 0 else None)
        if c == 0:
            rho_out[...] = rho
            rho_copy.start()
        store_aux(c, rho, pressure(rho, p_ref[c, :, 6, :], live_t[c], sound), True)
    first_pass(last, own_pairs, False)
    rho = finish_density(last, None)
    store_aux(last, rho, pressure(rho, p_ref[last, :, 6, :], live_t[last], sound), True)

    for c in range(last):
        second_pass(c, own_pairs, True)
    rho_copy.wait_recv()
    rho = rho_in[...]
    store_aux(n_cols, rho, pressure(rho, ghost[:, 6, :], live_t[n_cols], sound), False)
    second_pass(last, side_pairs, True)
    ghost_totals(acc_i2, part2_out)
    part2_copy.start()
    for c in range(last):
        second_pass(c, side_pairs, False)
    second_pass(last, own_pairs, False)
    finish_force(last, None, sound)
    part2_copy.wait_recv()
    for c in range(last):
        finish_force(c, part2_in if c == 0 else None, sound)

    for copy in [ghost_copy, count_copy, part1_copy, rho_copy, part2_copy] + near_copies + far_copies:
        copy.wait_send()


def on_device(sizes, particles, counts):
    n_group, n_dev, block = sizes
    blocks = n_group * n_dev // block
    n_cols, n_rows, comps, slots = particles.shape
    f32, bf16 = (jnp.float32, jnp.bfloat16)
    vmem = pl.BlockSpec(memory_space=pltpu.VMEM)
    pair_store = pltpu.VMEM((n_cols, n_rows, 5, slots, slots), f32)
    acc_i = pltpu.VMEM((n_cols + 1, n_rows + 2, 2, 8, slots), f32)
    acc_j = pltpu.VMEM((n_cols, n_rows, 2, slots, slots), f32)
    pair_rows = pltpu.VMEM((2, n_rows, slots), f32)
    return pl.pallas_call(
        functools.partial(body, sizes),
        out_shape=(
            jax.ShapeDtypeStruct((n_cols, n_rows, slots), f32),
            jax.ShapeDtypeStruct((n_cols, n_rows, slots), f32),
            jax.ShapeDtypeStruct((n_cols, n_rows, 2, slots), f32),
        ),
        in_specs=[vmem, vmem],
        out_specs=(vmem, vmem, vmem),
        scratch_shapes=[
            pltpu.VMEM((8, slots), f32),
            pltpu.VMEM((n_cols, n_rows, slots, slots), bf16),
            pltpu.VMEM((n_cols, n_rows, slots, slots), bf16),
            pltpu.VMEM((n_cols + 1, n_rows + 2, 5, 2, 3, 16, slots), bf16),
            pltpu.VMEM((n_cols + 1, n_rows + 2, 3, 3, 16, slots), bf16),
            pltpu.VMEM((n_cols + 1, n_rows + 2, 5, 2, 32, slots), bf16),
            pltpu.VMEM((n_cols + 1, n_rows + 2, 2, 32, slots), bf16),
            pltpu.VMEM((3, 5, slots, slots), f32),
            pltpu.VMEM((3, 4, slots, slots), f32),
            pltpu.VMEM((n_cols + 1, n_rows, slots), f32),
            pair_store,
            pair_store,
            acc_i,
            acc_j,
            acc_i,
            acc_j,
            pair_rows,
            pltpu.VMEM((n_rows, 8, slots), f32),
            pltpu.VMEM(counts.shape, jnp.int32),
            pair_rows,
            pair_rows,
            pltpu.VMEM((n_rows, slots), f32),
            pltpu.VMEM((n_rows, slots), f32),
            pair_rows,
            pair_rows,
            pltpu.VMEM((block, 8, slots), f32),
            pltpu.VMEM((blocks, 8, slots), f32),
            pltpu.VMEM((8, slots), f32),
            pltpu.VMEM((8, slots), f32),
            pltpu.SemaphoreType.DMA((5,)),
            pltpu.SemaphoreType.DMA((5,)),
            pltpu.SemaphoreType.DMA((block,)),
            pltpu.SemaphoreType.DMA((block,)),
            pltpu.SemaphoreType.DMA((blocks,)),
            pltpu.SemaphoreType.DMA((blocks,)),
        ],
        compiler_params=pltpu.CompilerParams(
            collective_id=0, has_side_effects=True, vmem_limit_bytes=60 * 1024 * 1024
        ),
        name="sph",
    )(particles, counts)


def solution(mesh):
    n_group, n_dev = (mesh.shape["group"], mesh.shape["dev"])
    block = 1
    while block * block * 4 <= n_group * n_dev:
        block *= 2
    return jax.shard_map(
        functools.partial(on_device, (n_group, n_dev, block)),
        mesh=mesh,
        in_specs=(P(("group", "dev"), None, None, None), P(("group", "dev"), None)),
        out_specs=(
            P(("group", "dev"), None, None),
            P(("group", "dev"), None, None),
            P(("group", "dev"), None, None, None),
        ),
        check_vma=False,
    )
```

```python
import functools
import math

import jax
import jax.numpy as jnp
from jax import lax
from jax.experimental import pallas as pl
from jax.experimental.pallas import tpu as pltpu
from jax.sharding import PartitionSpec as P

MESH = pl.DeviceIdType.MESH

kernel_scale = 28.0 / math.pi
gradient_scale = 140.0 / math.pi
sound_factor = 10.0
softening = 0.01 / 4.0
tiny = 1e-30

own_pairs = ((0, 0, 0), (1, 0, 1))
side_pairs = ((2, 1, -1), (3, 1, 0), (4, 1, 1))


def spread_row(row):
    return jnp.broadcast_to(row, (8, row.shape[1]))


def column_of(row):
    n = row.shape[1]
    eye = lax.broadcasted_iota(jnp.int32, (n, n), 0) == lax.broadcasted_iota(jnp.int32, (n, n), 1)
    return jnp.sum(jnp.where(eye, jnp.broadcast_to(row, (n, n)), 0.0), axis=1, keepdims=True)


def split(value):
    high = value.astype(jnp.bfloat16).astype(jnp.float32)
    rest = value - high
    middle = rest.astype(jnp.bfloat16).astype(jnp.float32)
    return (high, middle, rest - middle)


def body(
    sizes,
    p_ref,
    n_ref,
    den_ref,
    rate_ref,
    acc_ref,
    mean_t,
    lhs1,
    moved,
    fixed,
    rows_t,
    cols_t,
    aux_rows,
    aux_cols,
    live_t,
    grad_t,
    visc_t,
    acc_i1,
    acc_j1,
    acc_i2,
    acc_j2,
    total_t,
    ghost,
    ghost_n,
    part1_out,
    part1_in,
    rho_out,
    rho_in,
    part2_out,
    part2_in,
    top1,
    top2,
    top_out,
    top2_out,
    send_sem,
    recv_sem,
    top1_send,
    top1_recv,
    top2_send,
    top2_recv,
):
    n_group, n_dev, block = sizes
    total = n_group * n_dev
    blocks = total // block
    n_cols, n_rows, _, slots = p_ref.shape
    me = lax.axis_index("group") * n_dev + lax.axis_index("dev")

    def coords(flat):
        return (lax.div(flat, n_dev), lax.rem(flat, n_dev))

    right = coords(lax.rem(me + 1, total))
    left = coords(lax.rem(me + total - 1, total))
    offset = lax.rem(me, block)
    which = lax.div(me, block)
    near = [coords(which * block + lax.rem(offset + k, block)) for k in range(1, block)]
    far = [coords(lax.rem(which + k, blocks) * block + offset) for k in range(1, blocks)]

    barrier = pltpu.get_barrier_semaphore()
    for other in [left, right] + near + far:
        pl.semaphore_signal(barrier, inc=1, device_id=other, device_id_type=MESH)

    def copy_to(src, dst, send, recv, device):
        return pltpu.make_async_remote_copy(
            src_ref=src,
            dst_ref=dst,
            send_sem=send,
            recv_sem=recv,
            device_id=device,
            device_id_type=MESH,
        )

    ghost_copy = copy_to(p_ref.at[0], ghost, send_sem.at[0], recv_sem.at[0], left)
    count_copy = copy_to(n_ref, ghost_n, send_sem.at[1], recv_sem.at[1], left)
    part1_copy = copy_to(part1_out, part1_in, send_sem.at[2], recv_sem.at[2], right)
    rho_copy = copy_to(rho_out, rho_in, send_sem.at[3], recv_sem.at[3], left)
    part2_copy = copy_to(part2_out, part2_in, send_sem.at[4], recv_sem.at[4], right)

    lane_ids = lax.broadcasted_iota(jnp.int32, (n_rows, slots), 1).astype(jnp.float32)
    mass_row = lax.broadcasted_iota(jnp.int32, (8, slots), 0) == 4

    def live_of(counts_row):
        fill = column_of(counts_row.astype(jnp.float32))
        return jnp.where(lane_ids < fill, 1.0, 0.0)

    row_ids = lax.broadcasted_iota(jnp.int32, (8, slots), 0)
    zeros = jnp.zeros((8, slots), jnp.float32)
    zeros16 = jnp.zeros((16, slots), jnp.bfloat16)

    def pick(k, value, other):
        return jnp.where(row_ids == k, value, other)

    def pair_up(a, b):
        return jnp.concatenate([a, b], axis=0).astype(jnp.bfloat16)

    def load_cell(c, r, tile):
        live = spread_row(live_t[c, pl.ds(r, 1), :])
        tile = jnp.where(mass_row & (live < 0.5), 0.0, tile)
        return tile - mean_t[...]

    def own_terms(tile):
        weight = jnp.where(row_ids < 2, 1.0, pick(5, softening, 0.0))
        square = jnp.sum(tile * tile * weight, axis=0, keepdims=True)
        turned = pltpu.roll(tile, 6, axis=0)
        product = tile * turned
        work = product[0:1, :] + product[1:2, :]
        reach = tile[5:6, :]
        return (
            spread_row(square),
            spread_row(reach * reach),
            spread_row(work),
            spread_row(reach * tile[7:8, :]),
            turned,
        )

    def lane_side(c, row, tile, kinds):
        _, reach_sq, _, viscous, _ = own_terms(tile)
        reach, coeff = [spread_row(tile[k : k + 1, :]) for k in (5, 7)]
        plain = (
            pick(5, 2.0 * reach, pick(6, reach_sq, 0.0)),
            pick(5, coeff, pick(6, viscous, pick(7, reach, 0.0))),
        )
        rows_t[c, row] = tile
        for q, value in enumerate(plain):
            for level, part in enumerate(split(value)):
                extra = pick((1, 3)[q], 1.0, 0.0) if level == 0 else zeros
                fixed[c, row, q, level] = pair_up(part, extra)
        for slot, dc, dr in kinds:
            here = tile + pick(0, float(dc), pick(1, float(dr), 0.0))
            size, _, work, _, turned = own_terms(here)
            back = pltpu.roll(here, 2, axis=0)
            for_size = jnp.where(
                row_ids < 2,
                -2.0 * here,
                pick(5, (2.0 * softening) * here, pick(6, size, 0.0)),
            )
            for_work = jnp.where(
                row_ids < 2, -turned, jnp.where(row_ids < 4, -back, pick(6, work, 0.0))
            )
            for q, value in enumerate((for_size, for_work)):
                for level, part in enumerate(split(value)):
                    extra = pick(2 * q, 1.0, 0.0) if level == 0 else zeros
                    moved[c, row, slot, q, level] = pair_up(part, extra)

    def sublane_side(c, r, tile):
        size, reach_sq, work, viscous, _ = own_terms(tile)
        first = split(pick(6, 1.0, tile))
        second = split(
            pick(0, size, pick(1, reach_sq, pick(2, work, pick(3, viscous, 0.0))))
        )
        levels = [jnp.concatenate([a, b], axis=0) for a, b in zip(first, second)]
        stack = [levels[k] for k in (0, 0, 0, 1, 1, 2)]
        stack = stack + [jnp.zeros((slots - 96, slots), jnp.float32)]
        lhs1[c, r] = jnp.concatenate(stack, axis=0).T.astype(jnp.bfloat16)
        turned = tile.T
        for q, k in enumerate((0, 1, 4)):
            cols_t[c, r, q] = jnp.broadcast_to(turned[:, k : k + 1], (slots, slots))

    def first_rhs(c, row, slot):
        parts = []
        for q in range(4):
            if q < 2:
                levels = [moved[c, row, slot, q, k] for k in range(3)]
            else:
                levels = [fixed[c, row, q - 2, k] for k in range(3)]
            stack = [levels[k] for k in (0, 1, 2, 0, 1, 0)] + [zeros16] * ((slots - 96) // 16)
            parts.append(jnp.concatenate(stack, axis=0))
        return jnp.concatenate(parts, axis=1)

    for c in range(n_cols):
        live_t[c] = live_of(n_ref[c : c + 1, :])
    top = jnp.zeros((n_rows, slots), jnp.float32)
    count = jnp.zeros((n_rows, slots), jnp.float32)
    mean_x = jnp.zeros((n_rows, slots), jnp.float32)
    mean_y = jnp.zeros((n_rows, slots), jnp.float32)
    for c in range(n_cols):
        vx, vy = (p_ref[c, :, 2, :], p_ref[c, :, 3, :])
        live = live_t[c]
        top = jnp.maximum(top, jnp.where(live > 0.5, vx * vx + vy * vy, 0.0))
        count = count + live
        mean_x = mean_x + live * vx
        mean_y = mean_y + live * vy
    top_row = spread_row(jnp.max(top, axis=0, keepdims=True))

    def whole_sum(value):
        lanes = jnp.sum(value, axis=0, keepdims=True)
        return jnp.broadcast_to(jnp.sum(spread_row(lanes), axis=1, keepdims=True), (8, slots))

    share = 1.0 / jnp.maximum(whole_sum(count), 1.0)
    mean_t[...] = jnp.where(
        row_ids < 2,
        0.5,
        pick(2, whole_sum(mean_x) * share, pick(3, whole_sum(mean_y) * share, 0.0)),
    )
    kinds_of = {}
    for c in range(n_cols + 1):
        kinds = own_pairs if c == 0 else side_pairs if c == n_cols else own_pairs + side_pairs
        kinds_of[c] = kinds
    acc_i1[...] = jnp.zeros_like(acc_i1)
    acc_i2[...] = jnp.zeros_like(acc_i2)

    for c in range(n_cols):

        def own_cell(r, carry, c=c):
            tile = load_cell(c, r, p_ref[c, r])
            lane_side(c, r, tile, kinds_of[c])
            sublane_side(c, r, tile)
            return carry

        lax.fori_loop(0, n_rows, own_cell, 0, unroll=2)

    top_out[...] = top_row
    top1[offset] = top_row

    def run_pairs(c, own, store, use, clear):
        dc = 0 if own else 1
        last_row = n_rows - 1

        def one_row(r, carry):
            if own:
                use(c, r, 0, 0, r, None)
                use(c, r, 1, 0, r + 1, store)
            else:
                use(c, r + 1, 2, 1, r, store)
                use(c, r, 4, 1, r + 1, False)
                use(c, r + 1, 3, 1, r + 1, False)
            return carry

        if not own:
            use(c, 0, 3, 1, 0, store)
        lax.fori_loop(0, last_row, one_row, 0)
        if own:
            use(c, last_row, 0, 0, last_row, None)
            if store:
                clear[c, last_row] = jnp.zeros((2, slots, slots), jnp.float32)

    step_of = {slot: (dc, dr) for slot, dc, dr in own_pairs + side_pairs}

    def first_use(c, r, slot, dc, i_row, store):
        out = jnp.dot(
            lhs1[c, r], first_rhs(c + dc, i_row, slot), preferred_element_type=jnp.float32
        )
        mass_i = spread_row(rows_t[c + dc, i_row, 4:5, :])
        total_w = total_r = zeros
        for g in range(slots // 8):
            at = slice(g * 8, g * 8 + 8)
            size, closing, reach_sq, coeff = [out[at, q * slots : (q + 1) * slots] for q in range(4)]
            inv_sq = 1.0 / reach_sq
            ratio_sq = jnp.maximum(size * inv_sq - softening, tiny)
            ratio = ratio_sq * lax.rsqrt(ratio_sq)
            fall = jnp.maximum(1.0 - ratio, 0.0)
            base = fall * fall * fall * (inv_sq * (mass_i * cols_t[c, r, 2, at, :]))
            grad = base * inv_sq
            kern = base * (fall * (1.25 - fall))
            rate = closing * grad
            visc = jnp.minimum(rate, 0.0) * (coeff * (1.0 / size))
            grad_t[c, r, slot, at, :] = grad
            visc_t[c, r, slot, at, :] = visc
            total_w = total_w + kern
            total_r = total_r + rate
            if store:
                acc_j1[c, r, 0, at, :] = kern
                acc_j1[c, r, 1, at, :] = rate
            elif store is not None:
                acc_j1[c, r, 0, at, :] += kern
                acc_j1[c, r, 1, at, :] += rate
        acc_i1[c + dc, i_row, 0] += total_w
        acc_i1[c + dc, i_row, 1] += total_r

    def second_use(c, r, slot, dc, i_row, store):
        xi, yi = [
            spread_row(rows_t[c + dc, i_row, k : k + 1, :]) + float(step_of[slot][k])
            for k in range(2)
        ]
        rho_i, press_i = [spread_row(aux_rows[c + dc, i_row, k : k + 1, :]) for k in range(2)]
        total_x = total_y = zeros
        for g in range(slots // 8):
            at = slice(g * 8, g * 8 + 8)
            dx = xi - cols_t[c, r, 0, at, :]
            dy = yi - cols_t[c, r, 1, at, :]
            rho = rho_i + aux_cols[c, r, 0, at, :]
            press = press_i + aux_cols[c, r, 1, at, :]
            force = press * grad_t[c, r, slot, at, :] + visc_t[c, r, slot, at, :] * (1.0 / rho)
            fx, fy = (force * dx, force * dy)
            total_x = total_x + fx
            total_y = total_y + fy
            if store:
                acc_j2[c, r, 0, at, :] = fx
                acc_j2[c, r, 1, at, :] = fy
            elif store is not None:
                acc_j2[c, r, 0, at, :] += fx
                acc_j2[c, r, 1, at, :] += fy
        acc_i2[c + dc, i_row, 0] += total_x
        acc_i2[c + dc, i_row, 1] += total_y

    def first_pass(c, own, store):
        run_pairs(c, own, store, first_use, acc_j1)

    def second_pass(c, own, store):
        run_pairs(c, own, store, second_use, acc_j2)

    def cell_totals(c, acc_i, acc_j, sign):
        def one_row(r, carry):
            for k in range(2):
                other = acc_j[c, r, k].T.reshape(slots // 8, 8, slots).sum(axis=0)
                both = acc_i[c, r, k] + sign * other
                total_t[k, pl.ds(r, 1), :] = jnp.sum(both, axis=0, keepdims=True)
            return carry

        lax.fori_loop(0, n_rows, one_row, 0, unroll=4)

    def ghost_totals(acc_i, out):
        def one_row(r, carry):
            for k in range(2):
                out[k, pl.ds(r, 1), :] = jnp.sum(acc_i[n_cols, r, k], axis=0, keepdims=True)
            return carry

        lax.fori_loop(0, n_rows, one_row, 0, unroll=4)

    def store_aux(c, rho, press, own):
        total_t[0] = rho
        total_t[1] = press

        def one_row(r, carry):
            rows = [spread_row(total_t[k, pl.ds(r, 1), :]) for k in range(2)]
            tile = pick(0, rows[0], rows[1])
            aux_rows[c, r] = tile
            if own:
                turned = tile.T
                for k in range(2):
                    aux_cols[c, r, k] = jnp.broadcast_to(turned[:, k : k + 1], (slots, slots))
            return carry

        lax.fori_loop(0, n_rows, one_row, 0, unroll=4)

    def finish_density(c, extra):
        cell_totals(c, acc_i1, acc_j1, 1.0)
        live = live_t[c] > 0.5
        over_mass = 1.0 / p_ref[c, :, 4, :]
        w, rate = (total_t[0], total_t[1])
        if extra is not None:
            w, rate = (w + extra[0], rate + extra[1])
        rho = w * over_mass * kernel_scale
        den_ref[c] = jnp.where(live, rho, 0.0)
        rate_ref[c] = jnp.where(live, rate * over_mass * (-gradient_scale), 0.0)
        return jnp.where(live, rho, 1.0)

    def pressure(rho, rest, live, sound):
        return jnp.where(live > 0.5, (-2.0 * sound) * (rho - rest) / (rho * rho), 0.0)

    def finish_force(c, extra, sound):
        cell_totals(c, acc_i2, acc_j2, -1.0)
        live = live_t[c] > 0.5
        scale = (-0.5 * gradient_scale * sound) / p_ref[c, :, 4, :]
        for k in range(2):
            value = total_t[k]
            if extra is not None:
                value = value + extra[k]
            acc_ref[c, :, k, :] = jnp.where(live, value * scale, 0.0)

    last = n_cols - 1

    pl.semaphore_wait(barrier, 2 + len(near) + len(far))
    ghost_copy.start()
    count_copy.start()
    near_copies = [
        copy_to(top_out, top1.at[offset], top1_send.at[k], top1_recv.at[offset], other)
        for k, other in enumerate(near)
    ]
    for copy in near_copies:
        copy.start()

    for c in range(n_cols):
        if c < last:
            first_pass(c, True, True)

    for k in range(1, block):
        sender = lax.rem(offset + k, block)
        copy_to(top_out, top1.at[sender], top1_send.at[k - 1], top1_recv.at[sender], left).wait_recv()
    block_top = top1[0]
    for k in range(1, block):
        block_top = jnp.maximum(block_top, top1[k])
    top2_out[...] = block_top
    top2[which] = block_top
    far_copies = [
        copy_to(top2_out, top2.at[which], top2_send.at[k], top2_recv.at[which], other)
        for k, other in enumerate(far)
    ]
    for copy in far_copies:
        copy.start()

    ghost_copy.wait_recv()
    count_copy.wait_recv()
    inside = jnp.where(me < total - 1, 1.0, 0.0)
    live_t[n_cols] = live_of(ghost_n[0:1, :]) * inside

    def ghost_cell(r, carry):
        lane_side(n_cols, r, load_cell(n_cols, r, ghost[r]), kinds_of[n_cols])
        return carry

    lax.fori_loop(0, n_rows, ghost_cell, 0, unroll=2)

    first_pass(last, False, True)
    ghost_totals(acc_i1, part1_out)
    part1_copy.start()
    for c in range(last):
        first_pass(c, False, False)

    for k in range(1, blocks):
        sender = lax.rem(which + k, blocks)
        copy_to(top2_out, top2.at[sender], top2_send.at[k - 1], top2_recv.at[sender], left).wait_recv()
    all_top = top2[0]
    for k in range(1, blocks):
        all_top = jnp.maximum(all_top, top2[k])
    all_top = jnp.max(all_top, axis=1, keepdims=True)
    sound_col = sound_factor * jnp.sqrt(all_top)
    sound = jnp.broadcast_to(sound_col[0:1, :], (n_rows, slots))

    part1_copy.wait_recv()
    for c in range(last):
        rho = finish_density(c, part1_in if c == 0 else None)
        if c == 0:
            rho_out[...] = rho
            rho_copy.start()
        store_aux(c, rho, pressure(rho, p_ref[c, :, 6, :], live_t[c], sound), True)
    first_pass(last, True, False)
    rho = finish_density(last, None)
    store_aux(last, rho, pressure(rho, p_ref[last, :, 6, :], live_t[last], sound), True)

    for c in range(last):
        second_pass(c, True, True)
    rho_copy.wait_recv()
    rho = rho_in[...]
    store_aux(n_cols, rho, pressure(rho, ghost[:, 6, :], live_t[n_cols], sound), False)
    second_pass(last, False, True)
    ghost_totals(acc_i2, part2_out)
    part2_copy.start()
    for c in range(last):
        second_pass(c, False, False)
    second_pass(last, True, False)
    finish_force(last, None, sound)
    part2_copy.wait_recv()
    for c in range(last):
        finish_force(c, part2_in if c == 0 else None, sound)

    for copy in [ghost_copy, count_copy, part1_copy, rho_copy, part2_copy] + near_copies + far_copies:
        copy.wait_send()


def on_device(sizes, particles, counts):
    n_group, n_dev, block = sizes
    blocks = n_group * n_dev // block
    n_cols, n_rows, comps, slots = particles.shape
    f32, bf16 = (jnp.float32, jnp.bfloat16)
    vmem = pl.BlockSpec(memory_space=pltpu.VMEM)
    pair_store = pltpu.VMEM((n_cols, n_rows, 5, slots, slots), f32)
    acc_i = pltpu.VMEM((n_cols + 1, n_rows, 2, 8, slots), f32)
    acc_j = pltpu.VMEM((n_cols, n_rows, 2, slots, slots), f32)
    pair_rows = pltpu.VMEM((2, n_rows, slots), f32)
    return pl.pallas_call(
        functools.partial(body, sizes),
        out_shape=(
            jax.ShapeDtypeStruct((n_cols, n_rows, slots), f32),
            jax.ShapeDtypeStruct((n_cols, n_rows, slots), f32),
            jax.ShapeDtypeStruct((n_cols, n_rows, 2, slots), f32),
        ),
        in_specs=[vmem, vmem],
        out_specs=(vmem, vmem, vmem),
        scratch_shapes=[
            pltpu.VMEM((8, slots), f32),
            pltpu.VMEM((n_cols, n_rows, slots, slots), bf16),
            pltpu.VMEM((n_cols + 1, n_rows, 5, 2, 3, 16, slots), bf16),
            pltpu.VMEM((n_cols + 1, n_rows, 2, 3, 16, slots), bf16),
            pltpu.VMEM((n_cols + 1, n_rows, 8, slots), f32),
            pltpu.VMEM((n_cols, n_rows, 3, slots, slots), f32),
            pltpu.VMEM((n_cols + 1, n_rows, 8, slots), f32),
            pltpu.VMEM((n_cols, n_rows, 2, slots, slots), f32),
            pltpu.VMEM((n_cols + 1, n_rows, slots), f32),
            pair_store,
            pair_store,
            acc_i,
            acc_j,
            acc_i,
            acc_j,
            pair_rows,
            pltpu.VMEM((n_rows, 8, slots), f32),
            pltpu.VMEM(counts.shape, jnp.int32),
            pair_rows,
            pair_rows,
            pltpu.VMEM((n_rows, slots), f32),
            pltpu.VMEM((n_rows, slots), f32),
            pair_rows,
            pair_rows,
            pltpu.VMEM((block, 8, slots), f32),
            pltpu.VMEM((blocks, 8, slots), f32),
            pltpu.VMEM((8, slots), f32),
            pltpu.VMEM((8, slots), f32),
            pltpu.SemaphoreType.DMA((5,)),
            pltpu.SemaphoreType.DMA((5,)),
            pltpu.SemaphoreType.DMA((block,)),
            pltpu.SemaphoreType.DMA((block,)),
            pltpu.SemaphoreType.DMA((blocks,)),
            pltpu.SemaphoreType.DMA((blocks,)),
        ],
        compiler_params=pltpu.CompilerParams(
            collective_id=0, has_side_effects=True, vmem_limit_bytes=60 * 1024 * 1024
        ),
        name="sph",
    )(particles, counts)


def solution(mesh):
    n_group, n_dev = (mesh.shape["group"], mesh.shape["dev"])
    block = 1
    while block * block * 4 <= n_group * n_dev:
        block *= 2
    return jax.shard_map(
        functools.partial(on_device, (n_group, n_dev, block)),
        mesh=mesh,
        in_specs=(P(("group", "dev"), None, None, None), P(("group", "dev"), None)),
        out_specs=(
            P(("group", "dev"), None, None),
            P(("group", "dev"), None, None),
            P(("group", "dev"), None, None, None),
        ),
        check_vma=False,
    )
```
